32 devices in a mesh: site: 2 (over y), pts: 4 (over z), var: 2 (over x), cmp: 2 (over core).
Axes of the slice: x: 2, y: 2, z: 4, core: 2. Of those that a mesh axis runs over, the one named last changes fastest.
Arguments:
- sgt: bfloat16 [6, 3, 128, 4096], P('cmp', None, ('site', 'pts')), parts along dimension 2, may hold values from -6 to 6
- moment: float32 [6, 64], P('cmp', ('site', 'pts')), parts along dimension 1, may hold values from -6 to 6
- slip_spec: float32 [16, 2, 4096], replicated, may hold values from -3 to 3
- rp_slab: int32 [64], P('site'), parts along dimension 0, may hold values from 0 to 63, as said below
- rup_counts: int32 [8, 6], P(('site', 'pts')), parts along dimension 0, may hold values from 1 to 2, 8 in all within a row
- var_rupture: int32 [32], P('site'), parts along dimension 0, may hold values from 0 to 5
- var_source: int32 [32, 2], P('site'), parts along dimension 0, may hold values from 0 to 15
- owner_map: int32 [32], P('site'), parts along dimension 0, may hold values from 0 to 15, each once
Outputs:
- seismograms: float32 [32, 3, 4096], P(('site', 'pts', 'var', 'cmp')), parts along dimension 0
The draws below stay inside these ranges and needn't reach their ends.
There are 2 independent parts, one for each index of `site`. The reference program is written for one: setup_inputs(seed, part) draws one part's arguments, and reference() takes and returns one part's arrays. A program takes and returns all parts, laid end to end along the dimension named above; an argument that names none is the same for every part. Nothing has to cross between parts.
Inputs may be any that keep to these rules, and one draw needn't show every extreme that they name: `rp_slab`: in each aligned block of 8 rupture-points (one owner's), at most 4 name slab points of one reader (slab points k * 16 to (k + 1) * 16 - 1 belong to reader k), and in every block some reader is named exactly 4 times. `rup_counts`: each row gives, for the ruptures in order, how many of that owner's 8 slots belong to each; every rupture has 1 or more on every owner, the row sums to 8, and some entry of each row is exactly 2. `owner_map`: A permutation of the variations.
All inputs are finite; a program needn't handle non-finite values.
Results may differ from the reference program's by a relative error of at most 0.0003.
Values may be sent and summed in bfloat16 or wider, within the bound.
No kernel may reach another device: no remote copies, remote signals or barrier semaphores. Data moves between devices by JAX's collectives and lax.ppermute only.
A program may use at most 64 MiB of HBM per device.

```python
import math
import jax
import jax.numpy as jnp
import numpy as np
from jax import lax

NT = 4096
NMT = 6
NC = 3
TAU = 4
NSF = 16
NRUP = 6
RP_DEV = 8
SLAB_DEV = 16
MOSTP = 2
CAP = 4
OWNERS = 4
NRP = 32
NSLAB = 64
NVAR = 16


def draw_rp_slab(key, part):
    blocks = NRP // RP_DEV
    readers = NSLAB // SLAB_DEV
    pool_size = readers * CAP

    def one_block(block_key):
        key_first, key_scores, key_order, key_within = jax.random.split(block_key, 4)
        reader_of = jnp.arange(pool_size, dtype=jnp.int32) % readers
        first_reader = jax.random.randint(key_first, (), 0, readers, dtype=jnp.int32)
        scores = jax.random.randint(key_scores, (pool_size,), 0, 1 << 20, dtype=jnp.int32)
        scores = jnp.where(reader_of == first_reader, -1, scores)
        scores = scores * pool_size + jnp.arange(pool_size, dtype=jnp.int32)
        ordering = jnp.argsort(scores)
        chosen = reader_of[ordering][:RP_DEV]
        chosen = jax.random.permutation(key_order, chosen)
        within = jax.random.randint(key_within, (RP_DEV,), 0, SLAB_DEV, dtype=jnp.int32)
        return (chosen * SLAB_DEV + within).astype(jnp.int32)
    block_keys = jax.random.split(jax.random.fold_in(key, 17), blocks)
    return jax.vmap(one_block)(block_keys).reshape(NRP)


def touch_ends(entries, stream_key, smallest, top_value):
    index_at = [jax.random.randint(jax.random.fold_in(stream_key, axis), (), 0, length) for axis, length in enumerate(entries.shape)]
    longest = entries.shape.index(max(entries.shape))
    next_to = index_at[:longest] + [(index_at[longest] + 1) % entries.shape[longest]] + index_at[longest + 1:]
    return entries.at[tuple(index_at)].set(smallest).at[tuple(next_to)].set(top_value)


def level_of(key, shape, cuts, smallest, largest):
    def one(dim, blocks):
        draws = jax.random.uniform(jax.random.fold_in(jax.random.fold_in(key, 6), dim), (blocks,), jnp.float32, smallest / len(cuts), largest / len(cuts))
        return jnp.repeat(jnp.exp(draws), shape[dim] // blocks).reshape((-1,) + (1,) * (len(shape) - dim - 1))

    gain = one(*cuts[0])
    for cut in cuts[1:]:
        gain = gain * one(*cut)
    return gain


def rank_table(count, skew):
    weights = [(1 << 20) // math.isqrt(grade ** skew) + 1 for grade in range(1, count + 1)]
    scale = 1 + sum(weights) // (1 << 30)
    return np.cumsum(np.array([max(1, weight // scale) for weight in weights]))


def ranked(stream_key, dims, amount, slope):
    listing = rank_table(amount, slope)
    pick = jax.random.randint(jax.random.fold_in(stream_key, 1), dims, 0, int(listing[amount - 1]))
    rank = jnp.searchsorted(jnp.asarray(listing, jnp.int32), pick, side="right")
    return jax.random.permutation(jax.random.fold_in(stream_key, 2), amount)[rank].astype(jnp.int32)


def length_profile(number_of, total, bound, lean):
    loads = [(1 << 20) // math.isqrt(grade ** lean) + 1 for grade in range(2, number_of + 1)]
    rest, counts = total - bound - (number_of - 1), [1] * (number_of - 1)
    while rest > 0:
        movable = [i for i in range(number_of - 1) if counts[i] < bound]
        whole, left = sum([loads[i] for i in movable]), rest
        for i in movable:
            extra = min(bound - counts[i], max(1, left * loads[i] // whole), rest)
            counts[i] = counts[i] + extra
            rest = rest - extra
    return np.array([bound] + counts)


def ragged(stream_key, number_of, total, bound, slope):
    if number_of == 2:
        one = jax.random.randint(stream_key, (), max(1, total - bound), min(bound, total - 1) + 1)
        return jnp.stack([one, total - one])
    sizes = jnp.asarray(length_profile(number_of, total, bound, slope), jnp.int32)
    couples = (number_of - 1) // 2
    source_of, taker = sizes[1:1 + 2 * couples:2], sizes[2:2 + 2 * couples:2]
    slack = jnp.minimum(source_of - 1, bound - taker)
    moved = jax.random.randint(jax.random.fold_in(stream_key, 1), (couples,), 0, 1 << 20) % (slack + 1)
    sizes = sizes.at[1:1 + 2 * couples:2].set(source_of - moved).at[2:2 + 2 * couples:2].set(taker + moved)
    return sizes[jax.random.permutation(jax.random.fold_in(stream_key, 2), number_of)]


def normal_values(rng, shape, deviation, limit, cuts=(), held_as=jnp.bfloat16):
    values = jax.random.normal(rng, shape, jnp.float32) * deviation
    if len(cuts) > 0:
        values = level_of(rng, shape, cuts, -0.22, 0.18) * values
    return jnp.clip(values, min=-limit, max=limit).astype(held_as)


def setup_inputs(seed: int = 0, part: int = 0) -> dict:
    arg_keys = jax.random.split(jax.random.key(seed), 9)
    own_keys = jax.random.split(jax.random.fold_in(arg_keys[8], part), 9)
    return {
        "sgt": normal_values(own_keys[0], (NMT, NC, NSLAB, NT), 1.0, 6.0, ((0, 2), (2, 4))),
        "moment": normal_values(own_keys[1], (NMT, NRP), 0.4, 6.0, ((0, 2), (1, 4)), jnp.float32),
        "slip_spec": normal_values(arg_keys[2], (NSF, 2, NT), 0.2, 3.0, (), jnp.float32),
        "rp_slab": draw_rp_slab(jax.random.fold_in(jax.random.fold_in(arg_keys[8], part), 71), part),
        "rup_counts": jax.vmap(lambda own: ragged(own, NRUP, RP_DEV, MOSTP, 2))(jax.random.split(own_keys[4], OWNERS)).reshape((OWNERS, NRUP)).astype(jnp.int32),
        "var_rupture": touch_ends(ranked(own_keys[5], (NVAR,), NRUP, 2), jax.random.fold_in(own_keys[5], 3), 0, NRUP - 1).astype(jnp.int32),
        "var_source": touch_ends(jax.random.randint(own_keys[6], (NVAR, 2), 0, NSF), jax.random.fold_in(own_keys[6], 1), 0, NSF - 1).astype(jnp.int32),
        "owner_map": jax.random.permutation(own_keys[7], NVAR).astype(jnp.int32),
    }


def reference(sgt, moment, slip_spec, rp_slab, rup_counts, var_rupture, var_source, owner_map):
    samples = sgt.shape[3]
    length = 2 * samples
    owners = rup_counts.shape[0]
    rp_dev = rp_slab.shape[0] // owners
    functions = slip_spec.shape[0]

    def owner_spectra(owner_index):
        start_row = (owner_index * rp_dev).astype(jnp.int32)
        slab_rows = lax.dynamic_slice_in_dim(rp_slab, start_row, rp_dev, 0)
        weights = lax.dynamic_slice_in_dim(moment, start_row, rp_dev, 1)
        picked = jnp.take(sgt, slab_rows, axis=2).astype(jnp.float32)
        signal = jnp.sum(weights[:, None, :, None] * picked, axis=0)
        return jnp.fft.rfft(signal, n=length, axis=-1)[..., :samples]

    spectra = lax.map(owner_spectra, jnp.arange(owners, dtype=jnp.int32))
    spectra = jnp.moveaxis(spectra, 1, 2).reshape(owners * rp_dev, 3, samples)

    slot_iota = jnp.arange(rp_dev, dtype=jnp.int32)
    inclusive = jnp.cumsum(rup_counts, axis=1).astype(jnp.int32)
    rupture_of = jnp.sum(inclusive[:, None, :] <= slot_iota[None, :, None], axis=2).astype(jnp.int32)
    before = (jnp.cumsum(rup_counts, axis=0) - rup_counts).astype(jnp.int32)
    start_here = (inclusive - rup_counts).astype(jnp.int32)
    position = slot_iota[None, :] - jnp.take_along_axis(start_here, rupture_of, 1) + jnp.take_along_axis(before, rupture_of, 1)
    rupture_flat = rupture_of.reshape(-1)
    position_flat = position.reshape(-1).astype(jnp.int32)
    lengths = jnp.sum(rup_counts, axis=0).astype(jnp.int32)
    frequency = jnp.arange(samples, dtype=jnp.int32)

    def one_slot(slot_index):
        variation = owner_map[slot_index]
        rupture = var_rupture[variation]
        hypocenter = (var_source[variation, 0] * lengths[rupture]) // functions
        delays = (TAU * jnp.abs(position_flat - hypocenter)).astype(jnp.int32)
        numerator = (delays[:, None] * frequency[None, :]) % length
        angles = numerator.astype(jnp.float32) * (2.0 * math.pi / length)
        members = (rupture_flat == rupture).astype(jnp.float32)
        phases = (jnp.cos(angles) - 1j * jnp.sin(angles)) * members[:, None]
        summed = jnp.einsum("qf,qcf->cf", phases, spectra, precision=lax.Precision.HIGHEST)
        slip_rows = slip_spec[var_source[variation, 1]]
        product_spec = summed * (slip_rows[0] + 1j * slip_rows[1])[None, :]
        padded = jnp.concatenate([jnp.real(product_spec[:, :1]) + 0.0 * product_spec[:, :1], product_spec[:, 1:], jnp.zeros_like(product_spec[:, :1])], axis=1)
        return jnp.fft.irfft(padded, n=length, axis=-1)[:, :samples].astype(jnp.float32)

    return lax.map(one_slot, jnp.arange(owner_map.shape[0], dtype=jnp.int32))
```

```python
import math

import jax
import jax.numpy as jnp
import numpy as np
from jax import lax
from jax.experimental import pallas as pl
from jax.experimental.pallas import tpu as pltpu
from jax.sharding import PartitionSpec as P

TAU = 4
MOSTP = 2
LANES = 128

highest = lax.Precision.HIGHEST


def unit_tables(numerator, period):
    angles = (numerator % period).astype(np.float64) * (2.0 * math.pi / period)
    return np.cos(angles), np.sin(angles)


def transform_tables(comps, rows_in, samples):
    length = 2 * samples
    blocks = length // LANES
    rows_out = blocks // 2
    outer = np.arange(blocks)
    lane = np.arange(LANES)
    half = np.concatenate([np.arange(0, 64, 2), np.arange(1, 64, 2)])
    c1, s1 = unit_tables(outer[:, None] * np.arange(rows_in)[None, :], blocks)
    first = np.concatenate([c1, -s1], axis=0)
    first = np.kron(np.eye(comps), first)
    tc, ts = unit_tables(outer[:, None] * lane[None, :], length)
    c2, s2 = unit_tables(lane[:, None] * half[None, :], 128)
    real_cols = np.concatenate([c2, s2], axis=0)
    imag_cols = np.concatenate([-s2, c2], axis=0)
    second = np.concatenate([real_cols, imag_cols, -imag_cols, real_cols], axis=1)
    c3, s3 = c2.T, s2.T
    third = np.concatenate(
        [np.concatenate([c3, s3], axis=1), np.concatenate([-s3, c3], axis=1)], axis=0
    )
    c4, s4 = unit_tables(np.arange(rows_out)[:, None] * outer[None, :], blocks)
    last = np.concatenate([c4, -s4], axis=1)
    weights = np.full((blocks, 2 * half.size), 2.0 / length)
    weights[0, 0] = weights[0, half.size] = 1.0 / length
    return [np.asarray(x, np.float32) for x in (first, tc, ts, second, third, last, weights)]


def split_two(x):
    high = x.astype(jnp.bfloat16)
    low = (x - high.astype(jnp.float32)).astype(jnp.bfloat16)
    return high, low


def partial_kernel(
    slots, delays, ruptures, functions, var_count, cmp_count,
    table_s, rup_s, src_s, map_s, table_ref, slab_ref, sgt_ref, out_ref, lhs_ref,
):
    comp_half, slab_dev, samples = sgt_ref.shape
    group = out_ref.shape[0]
    rows = out_ref.shape[1] // pl.num_programs(1)
    points = slab_ref.shape[1]
    width = points // slots
    block = pl.program_id(0)
    comp = pl.program_id(1)

    @pl.when(comp == 0)
    def _():
        my_owner = lax.axis_index("pts")
        my_var = lax.axis_index("var")
        point = lax.broadcasted_iota(jnp.int32, (1, points), 1)
        rup_of = jnp.zeros((1, points), jnp.int32)
        pos = jnp.zeros((1, points), jnp.int32)
        lens = [jnp.int32(0)] * ruptures
        for o in range(slots):
            start = jnp.int32(o * width)
            for r in range(ruptures):
                count = table_s[comp_half, o * width + r].astype(jnp.int32)
                stop = start + count
                inside = (point >= start) & (point < stop)
                rup_of = jnp.where(inside, r, rup_of)
                pos = jnp.where(inside, point - start + lens[r], pos)
                lens[r] = lens[r] + count
                start = stop
        index = lax.broadcasted_iota(jnp.int32, (delays * group, 1), 0)
        member = index % group
        delay = index // group
        rup_col = jnp.zeros_like(index)
        hyp_col = jnp.zeros_like(index)
        for v in range(group):
            slot = block * group + v
            slot = ((slot // cmp_count) * var_count + my_var) * cmp_count + slot % cmp_count
            var_id = map_s[slot]
            rup = rup_s[var_id]
            length = lens[0]
            for r in range(1, ruptures):
                length = jnp.where(rup == r, lens[r], length)
            hyp = lax.div(src_s[2 * var_id] * length, jnp.int32(functions))
            rup_col = jnp.where(member == v, rup, rup_col)
            hyp_col = jnp.where(member == v, hyp, hyp_col)
        chosen = (rup_of == rup_col) & (jnp.abs(pos - hyp_col) == delay)
        chosen = chosen.astype(jnp.float32)
        row = lax.broadcasted_iota(jnp.int32, (slab_dev, 1), 0) + my_owner * slab_dev
        named = slab_ref[...] == row
        moments = jnp.concatenate(
            [jnp.where(named, table_ref[j:j + 1, :], 0.0) for j in range(comp_half)], axis=0
        )
        weights = lax.dot_general(
            chosen, moments, (((1,), (1,)), ((), ())),
            precision=highest, preferred_element_type=jnp.float32,
        )
        high, low = split_two(weights)
        inner = weights.shape[1]
        lhs_ref[:, :inner] = high
        lhs_ref[:, inner:] = low

    series = sgt_ref[...].reshape(comp_half * slab_dev, samples)
    series = jnp.concatenate([series, series], axis=0)
    product = jnp.dot(lhs_ref[...], series, preferred_element_type=jnp.float32)
    tail = jnp.zeros((group, rows * LANES - samples), jnp.float32)
    total = None
    for d in range(delays):
        piece = jnp.concatenate([product[d * group:(d + 1) * group], tail], axis=1)
        if d:
            piece = pltpu.roll(piece, TAU * d, 1)
        total = piece if total is None else total + piece
    for c in range(pl.num_programs(1)):
        @pl.when(comp == c)
        def _():
            for a in range(rows):
                out_ref[:, c * rows + a, :] = total[:, a * LANES:(a + 1) * LANES]


def finish_kernel(
    comps, var_count, cmp_count,
    src_s, map_s, parts_ref, first_ref, tc_ref, ts_ref, second_ref, third_ref, last_ref,
    weight_ref, slip_hbm, out_ref, slip_ref, sem,
):
    blocks = tc_ref.shape[0]
    rows_out = blocks // 2
    slot = lax.axis_index("pts") * var_count + lax.axis_index("var")
    slot = slot * cmp_count + lax.axis_index("cmp")
    function = src_s[2 * map_s[slot] + 1]
    copy = pltpu.make_async_copy(slip_hbm.at[function], slip_ref, sem)
    copy.start()
    signal = parts_ref[0]
    for p in range(1, parts_ref.shape[0]):
        signal = signal + parts_ref[p]
    dot = lambda a, b: jnp.dot(a, b, precision=highest, preferred_element_type=jnp.float32)
    first = dot(first_ref[...], signal)
    tc = tc_ref[...]
    ts = ts_ref[...]
    joined = []
    for c in range(comps):
        re = first[2 * c * blocks:(2 * c + 1) * blocks]
        im = first[(2 * c + 1) * blocks:(2 * c + 2) * blocks]
        joined.append(jnp.concatenate([re * tc + im * ts, im * tc - re * ts], axis=1))
    spectra = dot(jnp.concatenate(joined, axis=0), second_ref[...])
    copy.wait()
    slips = []
    for part in range(2):
        wide = jnp.concatenate(
            [slip_ref[part:part + 1, a * LANES:(a + 1) * LANES] for a in range(rows_out)], axis=0
        )
        turned = wide.T
        turned = jnp.concatenate([turned[:blocks], turned[blocks:]], axis=1)
        slips.append(jnp.concatenate([turned, turned], axis=1) * weight_ref[...])
    slips = [jnp.concatenate([s] * comps, axis=0) for s in slips]
    scaled = spectra[:, :LANES] * slips[0] + spectra[:, LANES:] * slips[1]
    middle = dot(scaled, third_ref[...])
    for c in range(comps):
        re = middle[c * blocks:(c + 1) * blocks, :LANES]
        im = middle[c * blocks:(c + 1) * blocks, LANES:]
        back = jnp.concatenate([re * tc - im * ts, re * ts + im * tc], axis=0)
        out_ref[c] = dot(last_ref[...], back)


def per_device(sgt, moment, slip_spec, rp_slab, rup_counts, var_rupture, var_source, owner_map):
    comp_half, comps, slab_dev, samples = sgt.shape
    rp_dev = moment.shape[1]
    owners = lax.axis_size("pts")
    var_count = lax.axis_size("var")
    cmp_count = lax.axis_size("cmp")
    ruptures = rup_counts.shape[1]
    functions = slip_spec.shape[0]
    targets = owners * cmp_count
    assert owner_map.shape[0] == targets * var_count and rp_dev >= ruptures
    delays = MOSTP * owners
    rows = -(-(samples + TAU * (delays - 1)) // LANES)
    group = 8 if targets % 8 == 0 else targets
    counts = jnp.pad(rup_counts.astype(jnp.float32), ((0, 0), (0, rp_dev - ruptures)))
    table = lax.all_gather(
        jnp.concatenate([moment, counts], axis=0), "pts", axis=1, tiled=True
    )
    points = rp_slab.shape[0]
    sources = var_source.reshape(-1)
    smem = pl.BlockSpec(memory_space=pltpu.SMEM)
    whole = lambda shape: pl.BlockSpec(shape, lambda *_: (0,) * len(shape))

    partial = pl.pallas_call(
        lambda *refs: partial_kernel(
            owners, delays, ruptures, functions, var_count, cmp_count, *refs
        ),
        grid=(targets // group, comps),
        in_specs=[
            smem, smem, smem, smem,
            whole(table.shape),
            whole((1, points)),
            pl.BlockSpec((comp_half, pl.squeezed, slab_dev, samples), lambda b, c: (0, c, 0, 0)),
        ],
        out_specs=pl.BlockSpec((group, comps * rows, LANES), lambda b, c: (b, 0, 0)),
        out_shape=jax.ShapeDtypeStruct((targets, comps * rows, LANES), jnp.float32),
        scratch_shapes=[pltpu.VMEM((delays * group, 2 * comp_half * slab_dev), jnp.bfloat16)],
    )
    parts = partial(
        table, var_rupture, sources, owner_map, table, rp_slab.reshape(1, points), sgt
    )
    parts = lax.all_to_all(parts, ("pts", "cmp"), split_axis=0, concat_axis=0, tiled=True)
    tables = transform_tables(comps, rows, samples)
    result = pl.pallas_call(
        lambda *refs: finish_kernel(comps, var_count, cmp_count, *refs),
        in_specs=[smem, smem]
        + [pl.BlockSpec(memory_space=pltpu.VMEM)] * (1 + len(tables))
        + [pl.BlockSpec(memory_space=pl.ANY)],
        out_specs=pl.BlockSpec(memory_space=pltpu.VMEM),
        out_shape=jax.ShapeDtypeStruct((comps, samples // LANES, LANES), jnp.float32),
        scratch_shapes=[pltpu.VMEM(slip_spec.shape[1:], jnp.float32), pltpu.SemaphoreType.DMA(())],
    )(sources, owner_map, parts, *tables, slip_spec)
    return result.reshape(1, comps, samples)


def solution(mesh):
    placed = (
        P("cmp", None, ("site", "pts"), None),
        P("cmp", ("site", "pts")),
        P(),
        P("site"),
        P(("site", "pts"), None),
        P("site"),
        P("site", None),
        P("site"),
    )
    return jax.shard_map(
        per_device,
        mesh=mesh,
        in_specs=placed,
        out_specs=P(("site", "pts", "var", "cmp"), None, None),
        check_vma=False,
    )
```

```python
import math

import jax
import jax.numpy as jnp
import numpy as np
from jax import lax
from jax.experimental import pallas as pl
from jax.experimental.pallas import tpu as pltpu
from jax.sharding import PartitionSpec as P

TAU = 4
MOSTP = 2
LANES = 128

highest = lax.Precision.HIGHEST


def unit_tables(numerator, period):
    angles = (numerator % period).astype(np.float64) * (2.0 * math.pi / period)
    return np.cos(angles), np.sin(angles)


def transform_tables(comps, rows_in, samples):
    length = 2 * samples
    blocks = length // LANES
    rows_out = blocks // 2
    outer = np.arange(blocks)
    lane = np.arange(LANES)
    half = np.concatenate([np.arange(0, 64, 2), np.arange(1, 64, 2)])
    c1, s1 = unit_tables(outer[:, None] * np.arange(rows_in)[None, :], blocks)
    first = np.concatenate([c1, -s1], axis=0)
    first = np.kron(np.eye(comps), first)
    tc, ts = unit_tables(outer[:, None] * lane[None, :], length)
    c2, s2 = unit_tables(lane[:, None] * half[None, :], 128)
    real_cols = np.concatenate([c2, s2], axis=0)
    imag_cols = np.concatenate([-s2, c2], axis=0)
    second = np.concatenate([real_cols, imag_cols, -imag_cols, real_cols], axis=1)
    c3, s3 = c2.T, s2.T
    third = np.concatenate(
        [np.concatenate([c3, s3], axis=1), np.concatenate([-s3, c3], axis=1)], axis=0
    )
    c4, s4 = unit_tables(np.arange(rows_out)[:, None] * outer[None, :], blocks)
    last = np.concatenate([c4, -s4], axis=1)
    turns = [np.asarray(x, np.float32) for x in (tc, ts)]
    return turns + [table_pair(x) for x in (first, second, third, last)]


def table_pair(x):
    high = x.astype(jnp.bfloat16)
    low = (x - high.astype(np.float64)).astype(jnp.bfloat16)
    return np.stack([high, low])


def reversed_bits(value, count):
    bits = count.bit_length() - 1
    total = 0
    for b in range(bits):
        total = total + (((value >> b) & 1) << (bits - 1 - b))
    return total


def split_two(x):
    high = x.astype(jnp.bfloat16)
    low = (x - high.astype(jnp.float32)).astype(jnp.bfloat16)
    return high, low


def partial_kernel(
    slots, delays, ruptures, functions, var_count, cmp_count, single,
    table_s, slab_s, rup_s, src_s, map_s, table_ref, sgt_ref, out_ref, lhs_ref,
):
    comp_half, slab_dev, samples = sgt_ref.shape
    group = out_ref.shape[0]
    rows = out_ref.shape[1] // pl.num_programs(1)
    points = slab_s.shape[0]
    width = points // slots
    block = 0 if single else pl.program_id(0)
    comp = pl.program_id(1)

    @pl.when(comp == 0)
    def _():
        my_owner = lax.axis_index("pts")
        my_var = lax.axis_index("var")
        my_core = lax.axis_index("cmp")
        point = lax.broadcasted_iota(jnp.int32, (1, points), 1)
        rup_of = jnp.zeros((1, points), jnp.int32)
        pos = jnp.zeros((1, points), jnp.int32)
        slab = jnp.zeros((1, points), jnp.int32)
        lens = [jnp.int32(0)] * ruptures
        for o in range(slots):
            base = jnp.bitwise_xor(my_owner, o) * width
            start = base
            for l in range(width):
                slab = jnp.where(point == base + l, slab_s[o * width + l], slab)
            for r in range(ruptures):
                count = table_s[comp_half, base + r].astype(jnp.int32)
                stop = start + count
                inside = (point >= start) & (point < stop)
                rup_of = jnp.where(inside, r, rup_of)
                pos = jnp.where(inside, point - start + lens[r], pos)
                lens[r] = lens[r] + count
                start = stop
        index = lax.broadcasted_iota(jnp.int32, (delays * group, 1), 0)
        member = index % group
        delay = index // group
        rup_col = jnp.zeros_like(index)
        hyp_col = jnp.zeros_like(index)
        for v in range(group):
            piece = block * group + v
            owner = jnp.bitwise_xor(my_owner, reversed_bits(piece % slots, slots))
            slot = (owner * var_count + my_var) * cmp_count
            slot = slot + jnp.bitwise_xor(my_core, piece // slots)
            var_id = map_s[slot]
            rup = rup_s[var_id]
            length = lens[0]
            for r in range(1, ruptures):
                length = jnp.where(rup == r, lens[r], length)
            hyp = lax.div(src_s[0, var_id] * length, jnp.int32(functions))
            rup_col = jnp.where(member == v, rup, rup_col)
            hyp_col = jnp.where(member == v, hyp, hyp_col)
        chosen = (rup_of == rup_col) & (jnp.abs(pos - hyp_col) == delay)
        chosen = chosen.astype(jnp.float32)
        row = lax.broadcasted_iota(jnp.int32, (slab_dev, 1), 0) + my_owner * slab_dev
        named = slab == row
        moments = jnp.concatenate(
            [jnp.where(named, table_ref[j:j + 1, :], 0.0) for j in range(comp_half)], axis=0
        )
        weights = lax.dot_general(
            chosen, moments, (((1,), (1,)), ((), ())),
            precision=highest, preferred_element_type=jnp.float32,
        )
        high, low = split_two(weights)
        inner = weights.shape[1]
        lhs_ref[:, :inner] = high
        lhs_ref[:, inner:] = low

    series = sgt_ref[...].reshape(comp_half * slab_dev, samples)
    series = jnp.concatenate([series, series], axis=0)
    product = jnp.dot(lhs_ref[...], series, preferred_element_type=jnp.float32)
    tail = jnp.zeros((group, rows * LANES - samples), jnp.float32)
    total = None
    for d in range(delays):
        piece = jnp.concatenate([product[d * group:(d + 1) * group], tail], axis=1)
        if d:
            piece = pltpu.roll(piece, TAU * d, 1)
        total = piece if total is None else total + piece
    for c in range(pl.num_programs(1)):
        @pl.when(comp == c)
        def _():
            for a in range(rows):
                out_ref[:, c * rows + a, :] = total[:, a * LANES:(a + 1) * LANES]


def slip_kernel(var_count, cmp_count, src_s, map_s, slip_hbm, out_ref, slip_ref, sem):
    blocks = out_ref.shape[1]
    rows_out = blocks // 2
    length = LANES * blocks
    slot = lax.axis_index("pts") * var_count + lax.axis_index("var")
    slot = slot * cmp_count + lax.axis_index("cmp")
    function = src_s[1, map_s[slot]]
    copy = pltpu.make_async_copy(slip_hbm.at[function], slip_ref, sem)
    copy.start()
    row = lax.broadcasted_iota(jnp.int32, (blocks, LANES), 0)
    lane = lax.broadcasted_iota(jnp.int32, (blocks, LANES), 1)
    steady = (row == 0) & (lane % (LANES // 2) == 0)
    weight = jnp.where(steady, 1.0 / length, 2.0 / length)
    copy.wait()
    for part in range(2):
        wide = jnp.concatenate(
            [slip_ref[part:part + 1, a * LANES:(a + 1) * LANES] for a in range(rows_out)], axis=0
        )
        turned = wide.T
        turned = jnp.concatenate([turned[:blocks], turned[blocks:]], axis=1)
        out_ref[part] = jnp.concatenate([turned, turned], axis=1) * weight


def dot_pairs(a, b):
    dot = lambda x, y: jnp.dot(x, y, preferred_element_type=jnp.float32)
    return dot(a[0], b[0]) + (dot(a[0], b[1]) + dot(a[1], b[0]))


def finish_kernel(
    comps, kept_ref, came_ref, slip_ref, tc_ref, ts_ref, first_ref, second_ref, third_ref,
    last_ref, out_ref,
):
    blocks = tc_ref.shape[0]
    signal = kept_ref[0] + came_ref[0]
    first = dot_pairs(first_ref, split_two(signal))
    tc = tc_ref[...]
    ts = ts_ref[...]
    joined = []
    for c in range(comps):
        re = first[2 * c * blocks:(2 * c + 1) * blocks]
        im = first[(2 * c + 1) * blocks:(2 * c + 2) * blocks]
        joined.append(jnp.concatenate([re * tc + im * ts, im * tc - re * ts], axis=1))
    spectra = dot_pairs(split_two(jnp.concatenate(joined, axis=0)), second_ref)
    slips = [jnp.concatenate([slip_ref[part]] * comps, axis=0) for part in range(2)]
    scaled = spectra[:, :LANES] * slips[0] + spectra[:, LANES:] * slips[1]
    middle = dot_pairs(split_two(scaled), third_ref)
    for c in range(comps):
        re = middle[c * blocks:(c + 1) * blocks, :LANES]
        im = middle[c * blocks:(c + 1) * blocks, LANES:]
        back = jnp.concatenate([re * tc - im * ts, re * ts + im * tc], axis=0)
        out_ref[c] = dot_pairs(last_ref, split_two(back))


def per_device(sgt, moment, slip_spec, rp_slab, rup_counts, var_rupture, var_source, owner_map):
    comp_half, comps, slab_dev, samples = sgt.shape
    rp_dev = moment.shape[1]
    owners = lax.axis_size("pts")
    var_count = lax.axis_size("var")
    cmp_count = lax.axis_size("cmp")
    ruptures = rup_counts.shape[1]
    functions = slip_spec.shape[0]
    targets = owners * cmp_count
    assert owner_map.shape[0] == targets * var_count and rp_dev >= ruptures
    assert cmp_count == 2 and owners & (owners - 1) == 0
    delays = MOSTP * owners
    rows = -(-(samples + TAU * (delays - 1)) // LANES)
    group = 8 if targets % 8 == 0 else targets
    counts = jnp.pad(
        rup_counts.astype(jnp.float32), ((comp_half, 0), (0, rp_dev - ruptures))
    )
    table = jnp.pad(moment, ((0, 1), (0, 0))) + counts
    bits = [1 << b for b in range(owners.bit_length() - 1)]
    swap = lambda x, axis, size, bit: lax.ppermute(x, axis, [(i, i ^ bit) for i in range(size)])
    for bit in bits:
        table = jnp.concatenate([table, swap(table, "pts", owners, bit)], axis=1)
    sources = var_source.T
    smem = pl.BlockSpec(memory_space=pltpu.SMEM)
    vmem = pl.BlockSpec(memory_space=pltpu.VMEM)

    slips = pl.pallas_call(
        lambda *refs: slip_kernel(var_count, cmp_count, *refs),
        in_specs=[smem, smem, pl.BlockSpec(memory_space=pl.ANY)],
        out_specs=vmem,
        out_shape=jax.ShapeDtypeStruct((2, 2 * samples // LANES, LANES), jnp.float32),
        scratch_shapes=[pltpu.VMEM(slip_spec.shape[1:], jnp.float32), pltpu.SemaphoreType.DMA(())],
    )(sources, owner_map, slip_spec)

    partial = pl.pallas_call(
        lambda *refs: partial_kernel(
            owners, delays, ruptures, functions, var_count, cmp_count, targets == group, *refs
        ),
        grid=(targets // group, comps),
        in_specs=[
            smem, smem, smem, smem, smem,
            pl.BlockSpec(table.shape, lambda b, c: (0, 0)),
            pl.BlockSpec((comp_half, pl.squeezed, slab_dev, samples), lambda b, c: (0, c, 0, 0)),
        ],
        out_specs=pl.BlockSpec((group, comps * rows, LANES), lambda b, c: (b, 0, 0)),
        out_shape=jax.ShapeDtypeStruct((targets, comps * rows, LANES), jnp.float32),
        scratch_shapes=[pltpu.VMEM((delays * group, 2 * comp_half * slab_dev), jnp.bfloat16)],
    )
    kept = partial(table, rp_slab, var_rupture, sources, owner_map, table, sgt)
    came = None
    for axis, size, bit in [("cmp", cmp_count, 1)] + [("pts", owners, bit) for bit in bits]:
        if came is not None:
            kept = kept + came
        middle = kept.shape[0] // 2
        came = swap(kept[middle:], axis, size, bit)
        kept = kept[:middle]
    tables = transform_tables(comps, rows, samples)
    result = pl.pallas_call(
        lambda *refs: finish_kernel(comps, *refs),
        in_specs=[vmem] * (3 + len(tables)),
        out_specs=vmem,
        out_shape=jax.ShapeDtypeStruct((comps, samples // LANES, LANES), jnp.float32),
    )(kept, came, slips, *tables)
    return result.reshape(1, comps, samples)


def solution(mesh):
    placed = (
        P("cmp", None, ("site", "pts"), None),
        P("cmp", ("site", "pts")),
        P(),
        P("site"),
        P(("site", "pts"), None),
        P("site"),
        P("site", None),
        P("site"),
    )
    return jax.shard_map(
        per_device,
        mesh=mesh,
        in_specs=placed,
        out_specs=P(("site", "pts", "var", "cmp"), None, None),
        check_vma=False,
    )
```

```python
import math

import jax
import jax.numpy as jnp
import numpy as np
from jax import lax
from jax.experimental import pallas as pl
from jax.experimental.pallas import tpu as pltpu
from jax.sharding import PartitionSpec as P

TAU = 4
MOSTP = 2
LANES = 128

highest = lax.Precision.HIGHEST


def unit_tables(numerator, period):
    angles = (numerator % period).astype(np.float64) * (2.0 * math.pi / period)
    return np.cos(angles), np.sin(angles)


def transform_tables(comps, rows_in, samples):
    length = 2 * samples
    blocks = length // LANES
    rows_out = blocks // 2
    outer = np.arange(blocks)
    lane = np.arange(LANES)
    half = np.concatenate([np.arange(0, 64, 2), np.arange(1, 64, 2)])
    c1, s1 = unit_tables(outer[:, None] * np.arange(rows_in)[None, :], blocks)
    first = np.concatenate([c1, -s1], axis=0)
    first = np.kron(np.eye(comps), first)
    tc, ts = unit_tables(outer[:, None] * lane[None, :], length)
    c2, s2 = unit_tables(lane[:, None] * half[None, :], 128)
    real_cols = np.concatenate([c2, s2], axis=0)
    imag_cols = np.concatenate([-s2, c2], axis=0)
    second = np.concatenate([real_cols, imag_cols, -imag_cols, real_cols], axis=1)
    c3, s3 = c2.T, s2.T
    third = np.concatenate(
        [np.concatenate([c3, s3], axis=1), np.concatenate([-s3, c3], axis=1)], axis=0
    )
    c4, s4 = unit_tables(np.arange(rows_out)[:, None] * outer[None, :], blocks)
    last = np.concatenate([c4, -s4], axis=1)
    turns = [np.asarray(x, np.float32) for x in (tc, ts)]
    return turns + [table_pair(x) for x in (first, second, third, last)]


def table_pair(x):
    high = x.astype(jnp.bfloat16)
    low = (x - high.astype(np.float64)).astype(jnp.bfloat16)
    return np.stack([high, low])


def reversed_bits(value, count):
    bits = count.bit_length() - 1
    total = 0
    for b in range(bits):
        total = total + (((value >> b) & 1) << (bits - 1 - b))
    return total


def split_two(x):
    high = x.astype(jnp.bfloat16)
    low = (x - high.astype(jnp.float32)).astype(jnp.bfloat16)
    return high, low


def partial_kernel(
    slots, delays, ruptures, functions, var_count, cmp_count, single,
    slab_s, rup_s, src_s, map_s, table_ref, sgt_ref, kept_ref, sent_ref, lhs_ref, table_s, sem,
):
    comp_half, comps, slab_dev, samples = sgt_ref.shape
    group = 2 * slots if single else 8
    rows = kept_ref.shape[1] // comps
    points = slab_s.shape[0]
    width = points // slots
    block = 0 if single else pl.program_id(0)
    comp = pl.program_id(1)

    @pl.when(comp == 0)
    def _():
        my_owner = lax.axis_index("pts")
        my_var = lax.axis_index("var")
        my_core = lax.axis_index("cmp")

        @pl.when(pl.program_id(0) == 0)
        def _():
            copy = pltpu.make_async_copy(table_ref, table_s, sem)
            copy.start()
            copy.wait()

        point = lax.broadcasted_iota(jnp.int32, (1, points), 1)
        rup_of = jnp.zeros((1, points), jnp.int32)
        pos = jnp.zeros((1, points), jnp.int32)
        slab = jnp.zeros((1, points), jnp.int32)
        lens = [jnp.int32(0)] * ruptures
        for o in range(slots):
            base = jnp.bitwise_xor(my_owner, o) * width
            start = base
            for l in range(width):
                slab = jnp.where(point == base + l, slab_s[o * width + l], slab)
            for r in range(ruptures):
                count = table_s[comp_half, base + r].astype(jnp.int32)
                stop = start + count
                inside = (point >= start) & (point < stop)
                rup_of = jnp.where(inside, r, rup_of)
                pos = jnp.where(inside, point - start + lens[r], pos)
                lens[r] = lens[r] + count
                start = stop
        index = lax.broadcasted_iota(jnp.int32, (delays * group, 1), 0)
        member = index % group
        delay = index // group
        rup_col = jnp.zeros_like(index)
        hyp_col = jnp.zeros_like(index)
        for v in range(group):
            piece = block * group + v
            owner = jnp.bitwise_xor(my_owner, reversed_bits(piece % slots, slots))
            slot = (owner * var_count + my_var) * cmp_count
            slot = slot + jnp.bitwise_xor(my_core, piece // slots)
            var_id = map_s[slot]
            rup = rup_s[var_id]
            length = lens[0]
            for r in range(1, ruptures):
                length = jnp.where(rup == r, lens[r], length)
            hyp = lax.div(src_s[0, var_id] * length, jnp.int32(functions))
            rup_col = jnp.where(member == v, rup, rup_col)
            hyp_col = jnp.where(member == v, hyp, hyp_col)
        chosen = (rup_of == rup_col) & (jnp.abs(pos - hyp_col) == delay)
        chosen = chosen.astype(jnp.float32)
        row = lax.broadcasted_iota(jnp.int32, (slab_dev, 1), 0) + my_owner * slab_dev
        named = slab == row
        moments = jnp.concatenate(
            [jnp.where(named, table_ref[j:j + 1, :], 0.0) for j in range(comp_half)], axis=0
        )
        weights = lax.dot_general(
            chosen, moments, (((1,), (1,)), ((), ())),
            precision=highest, preferred_element_type=jnp.float32,
        )
        high, low = split_two(weights)
        inner = weights.shape[1]
        lhs_ref[:, :inner] = high
        lhs_ref[:, inner:] = low

    series = sgt_ref[:, comp].reshape(comp_half * slab_dev, samples)
    series = jnp.concatenate([series, series], axis=0)
    product = jnp.dot(lhs_ref[...], series, preferred_element_type=jnp.float32)
    tail = jnp.zeros((group, rows * LANES - samples), jnp.float32)
    total = None
    for d in range(delays):
        piece = jnp.concatenate([product[d * group:(d + 1) * group], tail], axis=1)
        if d:
            piece = pltpu.roll(piece, TAU * d, 1)
        total = piece if total is None else total + piece
    for c in range(comps):
        @pl.when(comp == c)
        def _():
            for a in range(rows):
                store_pieces(block, group, slots, kept_ref, sent_ref, c * rows + a,
                             total[:, a * LANES:(a + 1) * LANES])


def store_pieces(block, group, slots, kept_ref, sent_ref, row, values):
    if group == 2 * slots:
        kept_ref[:, row, :] = values[:slots]
        sent_ref[:, row, :] = values[slots:]
    else:
        first = block * group

        @pl.when(first < slots)
        def _():
            kept_ref[pl.ds(first, group), row, :] = values

        @pl.when(first >= slots)
        def _():
            sent_ref[pl.ds(first - slots, group), row, :] = values


def prepare_kernel(
    var_count, cmp_count, src_s, map_s, slip_hbm, sgt_hbm, out_ref, sgt_ref, slip_ref, sem, sgt_sem
):
    load = pltpu.make_async_copy(sgt_hbm, sgt_ref, sgt_sem)
    load.start()
    blocks = out_ref.shape[1]
    rows_out = blocks // 2
    length = LANES * blocks
    slot = lax.axis_index("pts") * var_count + lax.axis_index("var")
    slot = slot * cmp_count + lax.axis_index("cmp")
    function = src_s[1, map_s[slot]]
    copy = pltpu.make_async_copy(slip_hbm.at[function], slip_ref, sem)
    copy.start()
    row = lax.broadcasted_iota(jnp.int32, (blocks, LANES), 0)
    lane = lax.broadcasted_iota(jnp.int32, (blocks, LANES), 1)
    steady = (row == 0) & (lane % (LANES // 2) == 0)
    weight = jnp.where(steady, 1.0 / length, 2.0 / length)
    copy.wait()
    for part in range(2):
        wide = jnp.concatenate(
            [slip_ref[part:part + 1, a * LANES:(a + 1) * LANES] for a in range(rows_out)], axis=0
        )
        turned = wide.T
        turned = jnp.concatenate([turned[:blocks], turned[blocks:]], axis=1)
        out_ref[part] = jnp.concatenate([turned, turned], axis=1) * weight
    load.wait()


def dot_pairs(a, b):
    dot = lambda x, y: jnp.dot(x, y, preferred_element_type=jnp.float32)
    return dot(a[0], b[0]) + (dot(a[0], b[1]) + dot(a[1], b[0]))


def finish_kernel(
    comps, kept_ref, came_ref, slip_ref, tc_ref, ts_ref, first_ref, second_ref, third_ref,
    last_ref, out_ref,
):
    blocks = tc_ref.shape[0]
    signal = kept_ref[0] + came_ref[0]
    first = dot_pairs(first_ref, split_two(signal))
    tc = tc_ref[...]
    ts = ts_ref[...]
    joined = []
    for c in range(comps):
        re = first[2 * c * blocks:(2 * c + 1) * blocks]
        im = first[(2 * c + 1) * blocks:(2 * c + 2) * blocks]
        joined.append(jnp.concatenate([re * tc + im * ts, im * tc - re * ts], axis=1))
    spectra = dot_pairs(split_two(jnp.concatenate(joined, axis=0)), second_ref)
    slips = [jnp.concatenate([slip_ref[part]] * comps, axis=0) for part in range(2)]
    scaled = spectra[:, :LANES] * slips[0] + spectra[:, LANES:] * slips[1]
    middle = dot_pairs(split_two(scaled), third_ref)
    for c in range(comps):
        re = middle[c * blocks:(c + 1) * blocks, :LANES]
        im = middle[c * blocks:(c + 1) * blocks, LANES:]
        back = jnp.concatenate([re * tc - im * ts, re * ts + im * tc], axis=0)
        out_ref[c] = dot_pairs(last_ref, split_two(back))


def per_device(sgt, moment, slip_spec, rp_slab, rup_counts, var_rupture, var_source, owner_map):
    comp_half, comps, slab_dev, samples = sgt.shape
    rp_dev = moment.shape[1]
    owners = lax.axis_size("pts")
    var_count = lax.axis_size("var")
    cmp_count = lax.axis_size("cmp")
    ruptures = rup_counts.shape[1]
    functions = slip_spec.shape[0]
    targets = owners * cmp_count
    assert owner_map.shape[0] == targets * var_count and rp_dev >= ruptures
    assert cmp_count == 2 and owners & (owners - 1) == 0
    delays = MOSTP * owners
    rows = -(-(samples + TAU * (delays - 1)) // LANES)
    group = 8 if owners % 8 == 0 else targets
    near = lambda x: pltpu.with_memory_space_constraint(x, pltpu.VMEM)
    far = lambda x: pltpu.with_memory_space_constraint(x, pltpu.HBM)
    counts = jnp.pad(
        rup_counts, ((comp_half, 0), (0, rp_dev - ruptures))
    ).astype(jnp.float32)
    table = jnp.pad(moment, ((0, 1), (0, 0))) + counts
    bits = [1 << b for b in range(owners.bit_length() - 1)]
    swap = lambda x, axis, size, bit: lax.ppermute(x, axis, [(i, i ^ bit) for i in range(size)])
    for bit in bits:
        table = jnp.concatenate([table, swap(table, "pts", owners, bit)], axis=1)
    sources = var_source.T
    smem = pl.BlockSpec(memory_space=pltpu.SMEM)
    vmem = pl.BlockSpec(memory_space=pltpu.VMEM)

    slips, series = pl.pallas_call(
        lambda *refs: prepare_kernel(var_count, cmp_count, *refs),
        in_specs=[smem, smem] + [pl.BlockSpec(memory_space=pltpu.HBM)] * 2,
        out_specs=[vmem] * 2,
        out_shape=[
            pltpu.VMEM((2, 2 * samples // LANES, LANES), jnp.float32),
            pltpu.VMEM(sgt.shape, sgt.dtype),
        ],
        scratch_shapes=[pltpu.VMEM(slip_spec.shape[1:], jnp.float32)]
        + [pltpu.SemaphoreType.DMA(())] * 2,
        compiler_params=pltpu.CompilerParams(vmem_limit_bytes=8 << 20),
    )(sources, owner_map, far(slip_spec), far(sgt))

    partial = pl.pallas_call(
        lambda *refs: partial_kernel(
            owners, delays, ruptures, functions, var_count, cmp_count, targets == group, *refs
        ),
        grid=(targets // group, comps),
        in_specs=[smem] * 4 + [vmem] * 2,
        out_specs=[vmem] * 2,
        out_shape=[pltpu.VMEM((owners, comps * rows, LANES), jnp.float32)] * 2,
        scratch_shapes=[
            pltpu.VMEM((delays * group, 2 * comp_half * slab_dev), jnp.bfloat16),
            pltpu.SMEM(table.shape, jnp.float32),
            pltpu.SemaphoreType.DMA(()),
        ],
        compiler_params=pltpu.CompilerParams(vmem_limit_bytes=40 << 20),
    )
    kept, sent = partial(rp_slab, var_rupture, sources, owner_map, near(table), near(series))
    came = None
    for axis, size, bit in [("cmp", cmp_count, 1)] + [("pts", owners, bit) for bit in bits]:
        if came is not None:
            total = kept + came
            middle = total.shape[0] // 2
            kept, sent = total[:middle], total[middle:]
        came = swap(sent, axis, size, bit)
    tables = transform_tables(comps, rows, samples)
    result = pl.pallas_call(
        lambda *refs: finish_kernel(comps, *refs),
        in_specs=[vmem] * (3 + len(tables)),
        out_specs=vmem,
        out_shape=jax.ShapeDtypeStruct((comps, samples // LANES, LANES), jnp.float32),
        compiler_params=pltpu.CompilerParams(vmem_limit_bytes=24 << 20),
    )(near(kept), near(came), near(slips), *[near(jnp.asarray(x)) for x in tables])
    return result.reshape(1, comps, samples)


def solution(mesh):
    placed = (
        P("cmp", None, ("site", "pts"), None),
        P("cmp", ("site", "pts")),
        P(),
        P("site"),
        P(("site", "pts"), None),
        P("site"),
        P("site", None),
        P("site"),
    )
    return jax.shard_map(
        per_device,
        mesh=mesh,
        in_specs=placed,
        out_specs=P(("site", "pts", "var", "cmp"), None, None),
        check_vma=False,
    )
```
